256 devices in a mesh: req: 64 (over y, x_lo, z), tp: 4 (over x_hi, core).
Axes of the slice: x: 4 (x_hi: 2, x_lo: 2; x = x_hi * 2 + x_lo), y: 4, z: 8, core: 2. Of those that a mesh axis runs over, the one named last changes fastest.
Arguments:
- queries: bfloat16 [65536, 2560], P('req', 'tp'), may hold values from -51 to 51
- fresh_keys: bfloat16 [65536, 2560], P('req', 'tp'), may hold values from -5 to 5
- fresh_values: bfloat16 [65536, 2560], P('req', 'tp'), may hold values from -24 to 24
- paged_keys: bfloat16 [1024, 128, 2560], P('req', None, 'tp'), may hold values from -6 to 6
- paged_values: bfloat16 [1024, 128, 2560], P('req', None, 'tp'), may hold values from -24 to 24
- request_page_table: int32 [512, 8], P('req'), may hold values from 0 to 15, as said below
- live_token_count: int32 [512], P('req'), may hold values from 2 to 128, as said below
- request_adapter_slot: int32 [512], P('req'), may hold values from 0 to 15
- adapters_in_use: int32 [16], replicated, may hold values from 0 to 63, as said below
- adapter_pool_row: int32 [64], replicated, may hold values from 0 to 63, each once
- adapter_down_factors: bfloat16 [64, 16, 2560], P('req', None, 'tp'), may hold values from -0.125 to 0.125
- adapter_up_factors: bfloat16 [64, 16, 2560], P('req'), may hold values from -1.5 to 1.5
- output_weight: bfloat16 [2560, 2560], P('tp'), may hold values from -0.125 to 0.125
- gating: float32 [512, 2560], P('req'), may hold values from 1 to 4
Outputs:
- gated: bfloat16 [65536, 2560], P(('req', 'tp'))
The draws below stay inside these ranges and needn't reach their ends.
Inputs may be any that keep to these rules, and one draw needn't show every extreme that they name: `request_page_table`: A request's 8 pages are distinct. `live_token_count`: some request has all 128 slots live. `adapters_in_use`: 16 distinct adapter ids.
All inputs are finite; a program needn't handle non-finite values.
Results may differ from the reference program's by a relative error of at most 0.0057.
Values may be sent and summed in bfloat16 or wider, within the bound.
A program may use at most 192 MiB of HBM per device.

```python
import math
import jax
import jax.numpy as jnp
import numpy as np
from jax import lax

HEADS = 20
HD = 128
OUTPUT_FEATURES = 2560
ADAPTER_RANK = 16
PAGE = 128
TOKENS_REQUEST = 128
PAGES_REQ = 8
REQ_DEV = 8
HEAD_FEATURES = 2560
REQUEST_TOTAL = 512
TOKENS = 65536
POOL_DEV = 16
POOL_PAGES = 1024
ADAPTER_TOTAL = 64
ACTIVE = 16


def paired_draw(key):
    base = jax.random.fold_in(key, 17)
    key_vals = jnp.clip(jax.random.normal(jax.random.fold_in(base, 1), (TOKENS, HEAD_FEATURES), jnp.float32), -5.0, 5.0)
    query_vals = jnp.clip(jax.random.normal(jax.random.fold_in(base, 2), (TOKENS, HEAD_FEATURES), jnp.float32), -5.0, 5.0)
    return (query_vals, key_vals)


def draw_queries(key, part):
    return paired_draw(key)[0].astype(jnp.bfloat16)


def draw_fresh_keys(key, part):
    return paired_draw(key)[1].astype(jnp.bfloat16)


def draw_request_page_table(key, part):
    request_keys = jax.random.split(jax.random.fold_in(key, 4), REQUEST_TOTAL)
    chosen = jax.vmap(lambda one_key: jax.random.permutation(one_key, POOL_DEV)[:PAGES_REQ])(request_keys)
    return chosen.astype(jnp.int32)


def draw_live_token_count(key, part):
    counts = jax.random.randint(jax.random.fold_in(key, 1), (REQUEST_TOTAL,), 2, TOKENS_REQUEST + 1)
    fullest = jax.random.randint(jax.random.fold_in(key, 2), (), 0, REQUEST_TOTAL)
    return jnp.where(jnp.arange(REQUEST_TOTAL) == fullest, TOKENS_REQUEST, counts).astype(jnp.int32)


def draw_adapters_in_use(key, part):
    middle = jax.random.permutation(jax.random.fold_in(key, 3), ADAPTER_TOTAL - 2)[:ACTIVE - 2].astype(jnp.int32) + 1
    ends = jnp.array([0, ADAPTER_TOTAL - 1], dtype=jnp.int32)
    listed = jnp.concatenate([ends, middle], axis=0)
    order = jax.random.permutation(jax.random.fold_in(key, 5), ACTIVE)
    return listed[order].astype(jnp.int32)


def plant(drawn, rng, smallest, top_value):
    spot = [jax.random.randint(jax.random.fold_in(rng, axis), (), 0, length) for axis, length in enumerate(drawn.shape)]
    longest = drawn.shape.index(max(drawn.shape))
    neighbour = spot[:longest] + [(spot[longest] + 1) % drawn.shape[longest]] + spot[longest + 1:]
    return drawn.at[tuple(spot)].set(smallest).at[tuple(neighbour)].set(top_value)


def shard_levels(own_key, extent, cuts, least, top_value):
    gain = 1.0
    for axis_at, shards_of in cuts:
        draws = jax.random.uniform(jax.random.fold_in(jax.random.fold_in(own_key, 6), axis_at), (shards_of,), jnp.float32, least / len(cuts), top_value / len(cuts))
        gain = gain * jnp.repeat(jnp.exp(draws), extent[axis_at] // shards_of).reshape((-1,) + (1,) * (len(extent) - 1 - axis_at))
    return gain


def rank_bounds(number_of, slope):
    weights = [(1 << 20) // math.isqrt(grade ** slope) + 1 for grade in range(1, number_of + 1)]
    spread = 1 + sum(weights) // (1 << 30)
    return np.cumsum(np.array([max(1, weight // spread) for weight in weights]))


def ranked_ids(key, shape, amount, skew):
    listing = rank_bounds(amount, skew)
    lot = jax.random.randint(jax.random.fold_in(key, 1), shape, 0, int(listing[amount - 1]))
    standing = jnp.searchsorted(jnp.asarray(listing, jnp.int32), lot, side="right")
    return jax.random.permutation(jax.random.fold_in(key, 2), amount)[standing].astype(jnp.int32)


def bell_draw(stream_key, shape, width, most, cuts=(), kind=jnp.bfloat16):
    factor_of = shard_levels(stream_key, shape, cuts, -0.22, 0.18) if cuts else 1.0
    result = jax.random.normal(stream_key, shape, jnp.float32) * width * factor_of
    return jnp.minimum(jnp.maximum(result, -most), most).astype(kind)


def setup_inputs(seed: int = 0) -> dict:
    arg_keys = jax.random.split(jax.random.key(seed), 15)
    queries = draw_queries(jax.random.fold_in(arg_keys[14], 71), 0)
    fresh_keys = draw_fresh_keys(jax.random.fold_in(arg_keys[14], 71), 0)
    fresh_values = bell_draw(arg_keys[2], (TOKENS, HEAD_FEATURES), 4.0, 24.0, ((0, 64), (1, 4)))
    paged_keys = bell_draw(arg_keys[3], (POOL_PAGES, PAGE, HEAD_FEATURES), 1.0, 6.0, ((0, 64), (2, 4)))
    paged_values = bell_draw(arg_keys[4], (POOL_PAGES, PAGE, HEAD_FEATURES), 4.0, 24.0, ((0, 64), (2, 4)))
    request_page_table = draw_request_page_table(jax.random.fold_in(arg_keys[14], 71), 0)
    live_token_count = draw_live_token_count(jax.random.fold_in(arg_keys[14], 71), 0)
    request_adapter_slot = plant(ranked_ids(arg_keys[7], (REQUEST_TOTAL,), ACTIVE, 2), jax.random.fold_in(arg_keys[7], 3), 0, ACTIVE - 1).astype(jnp.int32)
    adapters_in_use = draw_adapters_in_use(jax.random.fold_in(arg_keys[14], 71), 0)
    adapter_pool_row = jax.random.permutation(arg_keys[9], ADAPTER_TOTAL).astype(jnp.int32)
    adapter_down_factors = bell_draw(arg_keys[10], (ADAPTER_TOTAL, ADAPTER_RANK, HEAD_FEATURES), HEAD_FEATURES ** -0.5, 0.125, ((0, 64), (2, 4)))
    adapter_up_factors = bell_draw(arg_keys[11], (ADAPTER_TOTAL, ADAPTER_RANK, OUTPUT_FEATURES), ADAPTER_RANK ** -0.5, 1.5, ((0, 64),))
    output_weight = bell_draw(arg_keys[12], (HEAD_FEATURES, OUTPUT_FEATURES), HEAD_FEATURES ** -0.5, 0.125, ((0, 4),))
    gating = jnp.clip(jnp.exp(math.log(4.0) - 1.3862944 * jax.random.uniform(arg_keys[13], (REQUEST_TOTAL, OUTPUT_FEATURES), jnp.float32) ** shard_levels(arg_keys[13], (REQUEST_TOTAL, OUTPUT_FEATURES), ((0, 64),), -0.2, 0.2)), 1.0, 4.0)
    return dict(queries=queries, fresh_keys=fresh_keys, fresh_values=fresh_values, paged_keys=paged_keys, paged_values=paged_values, request_page_table=request_page_table, live_token_count=live_token_count, request_adapter_slot=request_adapter_slot, adapters_in_use=adapters_in_use, adapter_pool_row=adapter_pool_row, adapter_down_factors=adapter_down_factors, adapter_up_factors=adapter_up_factors, output_weight=output_weight, gating=gating)


def reference(queries, fresh_keys, fresh_values, paged_keys, paged_values, request_page_table, live_token_count, request_adapter_slot, adapters_in_use, adapter_pool_row, adapter_down_factors, adapter_up_factors, output_weight, gating):
    request_ids = jnp.arange(REQUEST_TOTAL, dtype=jnp.int32)
    page_rows = (request_ids // REQ_DEV * POOL_DEV)[:, None] + request_page_table.astype(jnp.int32)
    cached = PAGES_REQ * PAGE

    def attend_request(pieces):
        query, own_keys, own_values, page_index, token_count = pieces
        cached_keys = paged_keys[page_index].reshape(cached, HEAD_FEATURES)
        cached_values = paged_values[page_index].reshape(cached, HEAD_FEATURES)
        keys_all = jnp.concatenate([cached_keys, own_keys], axis=0).astype(jnp.float32).reshape(-1, HEADS, HD)
        values_all = jnp.concatenate([cached_values, own_values], axis=0).astype(jnp.float32).reshape(-1, HEADS, HD)
        query_heads = query.astype(jnp.float32).reshape(TOKENS_REQUEST, HEADS, HD)
        scores = jnp.einsum('qhd,khd->hqk', query_heads, keys_all, precision=lax.Precision.HIGHEST) * (1.0 / math.sqrt(HD))
        key_index = jnp.arange(cached + TOKENS_REQUEST, dtype=jnp.int32)
        usable = (key_index < cached) | (key_index - cached < token_count)
        scores = jnp.where(usable[None, None, :], scores, -1e+30)
        row_peak = lax.optimization_barrier(jnp.max(scores, axis=-1, keepdims=True))
        weights = jnp.exp(scores - row_peak)
        row_total = lax.optimization_barrier(jnp.sum(weights, axis=-1))
        rounded = weights.astype(jnp.bfloat16)
        blended = jnp.einsum('hqk,khd->qhd', rounded.astype(jnp.float32), values_all, precision=lax.Precision.HIGHEST)
        blended = blended / jnp.transpose(row_total)[:, :, None]
        live_slots = jnp.arange(TOKENS_REQUEST, dtype=jnp.int32) < token_count
        blended = jnp.where(live_slots[:, None, None], blended, 0.0)
        return blended.reshape(TOKENS_REQUEST, HEAD_FEATURES).astype(jnp.bfloat16)
    attention_output = lax.map(attend_request, (queries.reshape(REQUEST_TOTAL, TOKENS_REQUEST, HEAD_FEATURES), fresh_keys.reshape(REQUEST_TOTAL, TOKENS_REQUEST, HEAD_FEATURES), fresh_values.reshape(REQUEST_TOTAL, TOKENS_REQUEST, HEAD_FEATURES), page_rows, live_token_count.astype(jnp.int32)))
    adapter_rows = adapter_pool_row[adapters_in_use[request_adapter_slot]]
    down_factor_rows = adapter_down_factors[adapter_rows].astype(jnp.float32)
    up_factor_rows = adapter_up_factors[adapter_rows].astype(jnp.float32)
    rank_activations = jnp.einsum('rsh,rkh->rsk', attention_output.astype(jnp.float32), down_factor_rows, precision=lax.Precision.HIGHEST)
    adapter_term = jnp.einsum('zuh,zhd->zud', rank_activations, up_factor_rows, precision=lax.Precision.HIGHEST)
    projected_output = jnp.dot(attention_output.reshape(TOKENS, HEAD_FEATURES).astype(jnp.float32), output_weight.astype(jnp.float32), precision=lax.Precision.HIGHEST)
    adapter_update = projected_output.reshape(REQUEST_TOTAL, TOKENS_REQUEST, OUTPUT_FEATURES) + adapter_term
    gated = (gating[:, None, :] * adapter_update).astype(jnp.bfloat16)
    return gated.reshape(TOKENS, OUTPUT_FEATURES)
```

```python
import functools
import math

import jax
import jax.numpy as jnp
from jax import lax
from jax.experimental import pallas as pl
from jax.experimental.pallas import tpu as pltpu
from jax.sharding import PartitionSpec as P

HD = 128
RANK = 16
MESH = pl.DeviceIdType.MESH
NEG = -1e30
SCALE = math.log2(math.e) / math.sqrt(HD)
BF = jnp.bfloat16
F32 = jnp.float32
Y, XLO, Z = 4, 2, 8


def kernel(
    q_hbm, fk_hbm, fv_hbm, kp_hbm, vp_hbm, down_hbm, up_hbm, w_hbm, gate_hbm,
    pt, live, slot_of, in_use, pool_row,
    out_hbm,
    q, fk, fv, kp, vp, w, gate,
    att, psend, precv, pkeep, xsend, csend, crecv, acc, xrecv, stage,
    zbuf, ybuf, xbuf, slots, rbuf, ubuf, rsend, usend,
    lsem, osem,
    p_s, p_r, x_s, x_r, c_s, c_r, z_s, z_r, y_s, y_r, xl_s, xl_r, s_s, s_r, ra_s, ra_r, u_s, u_r,
):
    req = lax.axis_index("req")
    tp = lax.axis_index("tp")
    z = lax.rem(req, Z)
    yx = req // Z
    y = yx // XLO
    xlo = lax.rem(yx, XLO)
    hi = tp // 2
    core = lax.rem(tp, 2)
    width = q.shape[1]
    heads = width // HD
    n_out = w.shape[1]
    half = n_out // 2

    def at(y_, xlo_, z_):
        return (y_ * XLO + xlo_) * Z + z_

    partner = (req, hi * 2 + 1 - core)
    tp_peer = lambda d: (req, lax.rem(tp + d, 4))
    z_peer = lambda d: (at(y, xlo, lax.rem(z + d, Z)), tp)
    y_peer = lambda d: (at(lax.rem(y + d, Y), xlo, z), tp)
    xlo_peer = (at(y, 1 - xlo, z), tp)

    first = pl.multiple_of((1 - hi) * 512, 512)
    second = pl.multiple_of(hi * 512, 512)
    loads = []

    def load(src, dst):
        cp = pltpu.make_async_copy(src, dst, lsem.at[len(loads)])
        cp.start()
        loads.append(cp)
        return cp

    own_down = load(down_hbm.at[0], zbuf.at[0, pl.ds(0, RANK)])
    own_up = load(up_hbm.at[0, :, pl.ds(pl.multiple_of(tp * width, width), width)], zbuf.at[0, pl.ds(RANK, RANK)])
    early = [
        load(kp_hbm, kp),
        load(q_hbm.at[pl.ds(first, 512)], q.at[pl.ds(first, 512)]),
        load(fk_hbm.at[pl.ds(first, 512)], fk.at[pl.ds(first, 512)]),
        load(vp_hbm, vp),
        load(fv_hbm.at[pl.ds(first, 512)], fv.at[pl.ds(first, 512)]),
    ]
    load_w = load(w_hbm, w)
    late = [
        load(q_hbm.at[pl.ds(second, 512)], q.at[pl.ds(second, 512)]),
        load(fk_hbm.at[pl.ds(second, 512)], fk.at[pl.ds(second, 512)]),
        load(fv_hbm.at[pl.ds(second, 512)], fv.at[pl.ds(second, 512)]),
        load(gate_hbm, gate),
    ]

    barrier = pltpu.get_barrier_semaphore()
    peers = [tp_peer(d) for d in range(1, 4)] + [z_peer(d) for d in range(1, Z)]
    peers += [y_peer(d) for d in range(1, Y)] + [xlo_peer]
    for p in peers:
        pl.semaphore_signal(barrier, inc=1, device_id=p, device_id_type=MESH)
    pl.semaphore_wait(barrier, len(peers))

    def remote(src, dst, ss, rs, dev):
        return pltpu.make_async_remote_copy(src, dst, ss, rs, device_id=dev, device_id_type=MESH)

    z_copy = lambda d: remote(zbuf.at[0], zbuf.at[d], z_s.at[d], z_r.at[d], z_peer(d))
    y_copy = lambda d: remote(ybuf.at[0], ybuf.at[d], y_s.at[d], y_r.at[d], y_peer(d))
    xl_copy = lambda: remote(xbuf.at[0], xbuf.at[1], xl_s.at[0], xl_r.at[0], xlo_peer)
    s_copy = lambda d: remote(slots.at[0], slots.at[d], s_s.at[d], s_r.at[d], z_peer(d))

    own_down.wait()
    own_up.wait()
    for d in range(1, Z):
        z_copy(d).start()

    def phase_y():
        for d in range(1, Z):
            z_copy(d).wait_recv()
        for k in range(2):
            holder = pool_row[in_use[2 * z + k]]
            row = zbuf[lax.rem(z - lax.rem(holder, Z) + Z, Z)]
            ybuf[0, k] = jnp.where(holder // Z == yx, row.astype(F32), 0.0).astype(BF)
        for d in range(1, Y):
            y_copy(d).start()

    def phase_x():
        for d in range(1, Y):
            y_copy(d).wait_recv()
        total = ybuf[0].astype(F32) + ybuf[1].astype(F32) + ybuf[2].astype(F32) + ybuf[3].astype(F32)
        xbuf[0] = total.astype(BF)
        xl_copy().start()

    def phase_z():
        xl_copy().wait_recv()
        slots[0] = (xbuf[0].astype(F32) + xbuf[1].astype(F32)).astype(BF)
        for d in range(1, Z):
            s_copy(d).start()

    p_copy = lambda j: remote(psend.at[j], precv.at[j], p_s.at[j], p_r.at[j], partner)
    c_copy = lambda k: remote(csend.at[k], crecv.at[k], c_s.at[k], c_r.at[k], partner)

    def x_copy(j):
        return remote(
            xsend.at[j], xrecv.at[lax.rem(j, 2), core],
            x_s.at[j], x_r.at[lax.rem(j, 2), core],
            (req, (1 - hi) * 2 + j // 2),
        )

    def project(a, base, chunk):
        return jnp.dot(
            a, w[:, pl.ds(pl.multiple_of(base, 128), chunk)], preferred_element_type=F32
        )

    mine = pl.multiple_of(core * half, half)
    other = pl.multiple_of((1 - core) * half, half)
    CH = 640

    def pickup(j):
        p_copy(j).wait_recv()
        for n in range(0, half, CH):
            cols = pl.ds(n, CH)
            xsend[j, :, cols] = (pkeep[j, :, cols] + precv[j, :, cols].astype(F32)).astype(BF)
        x_copy(j).start()

    def request_of(step):
        there = (1 - hi) * 4 + step
        partners = hi * 4 + (1 - core) * 2 + step - 4
        own = hi * 4 + core * 2 + step - 6
        return jnp.where(step < 4, there, jnp.where(step < 6, partners, own))

    def head(r, h, pages, count):
        cols = pl.ds(h * HD, HD)
        rows = pl.ds(pl.multiple_of(r * 128, 128), 128)
        qh = q[rows, cols]
        contract = (((1,), (1,)), ((), ()))
        parts = []
        for g in range(0, 8, 2):
            k2 = jnp.concatenate([kp[pages[g], :, cols], kp[pages[g + 1], :, cols]], axis=0)
            parts.append(lax.dot_general(qh, k2, contract, preferred_element_type=F32))
        fresh = lax.dot_general(qh, fk[rows, cols], contract, preferred_element_type=F32)
        key_at = lax.broadcasted_iota(jnp.int32, fresh.shape, 1)
        parts.append(jnp.where(key_at < count, fresh, NEG))
        s = jnp.concatenate(parts, axis=1)
        peak = jnp.max(s, axis=1, keepdims=True)
        p = jnp.exp2((s - peak) * SCALE)
        total = jnp.sum(p, axis=1, keepdims=True)
        v = jnp.concatenate([vp[pages[g], :, cols] for g in range(8)] + [fv[rows, cols]], axis=0)
        o = jnp.dot(p.astype(BF), v, preferred_element_type=F32)
        o = o / total
        slot_at = lax.broadcasted_iota(jnp.int32, o.shape, 0)
        att[r, :, cols] = jnp.where(slot_at < count, o, 0.0).astype(BF)

    for cp in early:
        cp.wait()

    def step_body(step, carry):
        r = request_of(step)
        pages = [pt[r, g] for g in range(8)]
        count = live[r]

        @pl.when(step == 4)
        def _():
            for cp in late:
                cp.wait()

        for h in range(2):
            head(r, h, pages, count)

        @pl.when((step >= 1) & (step <= 4))
        def _():
            pickup(step - 1)

        for h in range(2, heads):
            head(r, h, pages, count)

        @pl.when(step == 0)
        def _():
            load_w.wait()

        a = att[r]

        @pl.when(step < 4)
        def _():
            for n in range(0, half, CH):
                psend[step, :, pl.ds(n, CH)] = project(a, other + n, CH).astype(BF)
            p_copy(step).start()
            for n in range(0, half, CH):
                pkeep[step, :, pl.ds(n, CH)] = project(a, mine + n, CH)

        @pl.when((step >= 4) & (step < 6))
        def _():
            for n in range(0, n_out, CH):
                csend[step - 4, :, pl.ds(n, CH)] = project(a, n, CH).astype(BF)
            c_copy(step - 4).start()

        @pl.when(step >= 6)
        def _():
            for n in range(0, n_out, CH):
                acc[step - 6, :, pl.ds(n, CH)] = project(a, n, CH)

        @pl.when(step == 0)
        def _():
            phase_y()

        @pl.when(step == 2)
        def _():
            phase_x()

        @pl.when(step == 3)
        def _():
            phase_z()

        return carry

    lax.fori_loop(0, 8, step_body, 0)

    for d in range(1, Z):
        s_copy(d).wait_recv()
    ra_copy = lambda d: remote(rsend.at[d], rbuf.at[d], ra_s.at[d], ra_r.at[d], tp_peer(d))
    u_copy = lambda d: remote(usend.at[d], ubuf.at[d], u_s.at[d], u_r.at[d], tp_peer(d))
    for d in (2, 3, 1, 0):
        for k in range(2):
            r = lax.rem(tp + d, 4) * 2 + k
            s = slot_of[r]
            place = lax.rem(z - s // 2 + Z, Z)
            factors = slots[place, lax.rem(s, 2)]
            ranked = lax.dot_general(
                factors[:RANK], att[r], (((1,), (1,)), ((), ())), preferred_element_type=F32
            )
            if d == 0:
                rbuf[0, k] = ranked
                ubuf[0, k] = factors[RANK:]
            else:
                rsend[d, k] = ranked
                usend[d, k] = factors[RANK:]
        if d:
            ra_copy(d).start()
            u_copy(d).start()

    for k in range(2):
        c_copy(k).wait_recv()
    for d in range(1, 4):
        ra_copy(d).wait_recv()
        u_copy(d).wait_recv()

    for k in range(2):
        ra = rbuf[0, k] + rbuf[1, k] + rbuf[2, k] + rbuf[3, k]
        top = ra.astype(BF)
        rest = ra - top.astype(F32)
        mid = rest.astype(BF)
        low = (rest - mid.astype(F32)).astype(BF)
        ra3 = jnp.concatenate([top, mid, low], axis=0)
        for n in range(4):
            cols = pl.ds(n * width, width)
            u1 = ubuf[lax.rem(tp - n + 4, 4), k]
            u3 = jnp.concatenate([u1, u1, u1], axis=0)
            term = lax.dot_general(ra3, u3, (((0,), (0,)), ((), ())), preferred_element_type=F32)
            acc[k, :, cols] = acc[k, :, cols] + crecv[k, :, cols].astype(F32) + term

    outs = []
    for k in range(2):
        g_row = tp * 2 + k
        for cs in range(2):
            remote(xsend.at[0], xrecv.at[k, cs], x_s.at[0], x_r.at[k, cs], partner).wait_recv()
            for n in range(0, half, CH):
                cols = pl.ds(cs * half + n, CH)
                total = acc[k, :, cols] + xrecv[k, cs, :, pl.ds(n, CH)].astype(F32)
                stage[k, :, cols] = (gate[pl.ds(g_row, 1), cols] * total).astype(BF)
            block = (pl.ds(k * 128, 128), pl.ds(cs * half, half))
            cp = pltpu.make_async_copy(
                stage.at[k, :, pl.ds(cs * half, half)], out_hbm.at[block], osem.at[k, cs]
            )
            cp.start()
            outs.append(cp)

    for d in range(1, Z):
        z_copy(d).wait_send()
        s_copy(d).wait_send()
    for d in range(1, Y):
        y_copy(d).wait_send()
    xl_copy().wait_send()
    for j in range(4):
        p_copy(j).wait_send()
        x_copy(j).wait_send()
    for k in range(2):
        c_copy(k).wait_send()
    for d in range(1, 4):
        ra_copy(d).wait_send()
        u_copy(d).wait_send()
    for cp in outs:
        cp.wait()


def body(
    queries, fresh_keys, fresh_values, paged_keys, paged_values, request_page_table,
    live_token_count, request_adapter_slot, adapters_in_use, adapter_pool_row,
    adapter_down_factors, adapter_up_factors, output_weight, gating,
):
    rows, width = queries.shape
    n_out = output_weight.shape[1]
    half = n_out // 2
    hbm = pl.BlockSpec(memory_space=pl.ANY)
    smem = pl.BlockSpec(memory_space=pltpu.SMEM)
    V = pltpu.VMEM
    dma = pltpu.SemaphoreType.DMA
    pair = (2, 2 * RANK, width)
    return pl.pallas_call(
        kernel,
        out_shape=jax.ShapeDtypeStruct((rows // 4, n_out), BF),
        in_specs=[hbm] * 9 + [smem] * 5,
        out_specs=hbm,
        scratch_shapes=[
            V((rows, width), BF), V((rows, width), BF), V((rows, width), BF),
            V(paged_keys.shape, BF), V(paged_values.shape, BF), V((width, n_out), BF), V(gating.shape, F32),
            V((8, 128, width), BF),
            V((4, 128, half), BF), V((4, 128, half), BF), V((4, 128, half), F32), V((4, 128, half), BF),
            V((2, 128, n_out), BF), V((2, 128, n_out), BF), V((2, 128, n_out), F32),
            V((2, 2, 128, half), BF), V((2, 128, n_out), BF),
            V((Z, 2 * RANK, width), BF), V((Y, *pair), BF), V((2, *pair), BF), V((Z, *pair), BF),
            V((4, 2, RANK, 128), F32), V((4, 2, RANK, width), BF),
            V((4, 2, RANK, 128), F32), V((4, 2, RANK, width), BF),
            dma((12,)), dma((2, 2)),
            dma((4,)), dma((4,)), dma((4,)), dma((2, 2)), dma((2,)), dma((2,)),
            dma((Z,)), dma((Z,)), dma((Y,)), dma((Y,)), dma((1,)), dma((1,)), dma((Z,)), dma((Z,)),
            dma((4,)), dma((4,)), dma((4,)), dma((4,)),
        ],
        compiler_params=pltpu.CompilerParams(
            collective_id=0, has_side_effects=True, vmem_limit_bytes=60 * 1024 * 1024
        ),
        name="attend_project",
    )(
        queries, fresh_keys, fresh_values, paged_keys, paged_values,
        adapter_down_factors, adapter_up_factors, output_weight, gating,
        request_page_table, live_token_count, request_adapter_slot, adapters_in_use, adapter_pool_row,
    )


def solution(mesh):
    return jax.shard_map(
        body,
        mesh=mesh,
        in_specs=(
            P("req", "tp"), P("req", "tp"), P("req", "tp"),
            P("req", None, "tp"), P("req", None, "tp"),
            P("req", None), P("req"), P("req"), P(), P(),
            P("req", None, "tp"), P("req", None, None), P("tp", None), P("req", None),
        ),
        out_specs=P(("req", "tp"), None),
        check_vma=False,
    )
```

```python
import functools
import math

import jax
import jax.numpy as jnp
from jax import lax
from jax.experimental import pallas as pl
from jax.experimental.pallas import tpu as pltpu
from jax.sharding import PartitionSpec as P

HD = 128
RANK = 16
MESH = pl.DeviceIdType.MESH
NEG = -1e30
SCALE = math.log2(math.e) / math.sqrt(HD)
BF = jnp.bfloat16
F32 = jnp.float32
Y, XLO, Z = 4, 2, 8
EVENTS = {
    (1, "b"): "sum", (4, "b"): "spread",
    (6, "a"): "f17", (6, "b"): "f26", (7, "a"): "f35", (7, "b"): "f4",
}


def kernel(
    q_hbm, fk_hbm, fv_hbm, kp_hbm, vp_hbm, down_hbm, up_hbm, w_hbm,
    pt, live, slot_of, in_use, pool_row,
    out,
    q, fk, fv, kp, vp, w,
    sbuf, pbuf, att, psend, precv, pkeep, xsend, csend, crecv, acc, xrecv,
    yrow, rs_send, rs_recv, gbuf, rbuf, ubuf, rsend, usend,
    lsem,
    p_s, p_r, x_s, x_r, c_s, c_r, y_s, y_r, z_s, z_r, g_s, g_r, f_s, f_r, ra_s, ra_r, u_s, u_r,
):
    req = lax.axis_index("req")
    tp = lax.axis_index("tp")
    z = lax.rem(req, Z)
    yx = req // Z
    y = yx // XLO
    xlo = lax.rem(yx, XLO)
    hi = tp // 2
    core = lax.rem(tp, 2)
    width = q.shape[1]
    heads = width // HD
    n_out = w.shape[1]
    half = n_out // 2

    def at(y_, xlo_, z_):
        return (y_ * XLO + xlo_) * Z + z_

    partner = (req, hi * 2 + 1 - core)
    tp_peer = lambda d: (req, lax.rem(tp + d, 4))
    z_peer = lambda d: (at(y, xlo, lax.rem(z + d, Z)), tp)
    y_peer = lambda d: (at(lax.rem(y + d, Y), xlo, z), tp)

    def plane_peer(e):
        return (at(lax.rem(y + e // 2, Y), lax.rem(xlo + e, 2), z), tp)


    first = pl.multiple_of((1 - hi) * 512, 512)
    second = pl.multiple_of(hi * 512, 512)
    loads = []

    def load(src, dst):
        cp = pltpu.make_async_copy(src, dst, lsem.at[len(loads)])
        cp.start()
        loads.append(cp)
        return cp

    own_down = load(down_hbm.at[0], yrow.at[0, pl.ds(0, RANK)])
    own_up = load(
        up_hbm.at[0, :, pl.ds(pl.multiple_of(tp * width, width), width)],
        yrow.at[0, pl.ds(RANK, RANK)],
    )
    early = [
        load(kp_hbm, kp),
        load(q_hbm.at[pl.ds(first, 512)], q.at[pl.ds(first, 512)]),
        load(fk_hbm.at[pl.ds(first, 512)], fk.at[pl.ds(first, 512)]),
        load(vp_hbm, vp),
        load(fv_hbm.at[pl.ds(first, 512)], fv.at[pl.ds(first, 512)]),
    ]
    load_w = load(w_hbm, w)
    late = [
        load(q_hbm.at[pl.ds(second, 512)], q.at[pl.ds(second, 512)]),
        load(fk_hbm.at[pl.ds(second, 512)], fk.at[pl.ds(second, 512)]),
        load(fv_hbm.at[pl.ds(second, 512)], fv.at[pl.ds(second, 512)]),
    ]

    barrier = pltpu.get_barrier_semaphore()
    peers = [tp_peer(d) for d in range(1, 4)] + [z_peer(d) for d in range(1, Z)]
    peers += [plane_peer(e) for e in range(1, Y * XLO)]
    for p in peers:
        pl.semaphore_signal(barrier, inc=1, device_id=p, device_id_type=MESH)
    pl.semaphore_wait(barrier, len(peers))

    def remote(src, dst, ss, rs, dev):
        return pltpu.make_async_remote_copy(src, dst, ss, rs, device_id=dev, device_id_type=MESH)

    def all_recv(buf, rs):
        remote(buf, buf, z_s.at[0], rs, partner).wait_recv()

    def all_sent(buf, ss):
        remote(buf, buf, ss, z_r.at[0], partner).wait_send()

    own_down.wait()
    own_up.wait()
    for e in range(1, Y * XLO):
        remote(yrow.at[0], yrow.at[e], y_s.at[0], y_r.at[0], plane_peer(e)).start()

    def phase_sum():
        all_recv(yrow.at[pl.ds(1, Y * XLO - 1)], y_r.at[0])
        for d in range(Z):
            p = lax.rem(z + d, Z)
            holder = pool_row[in_use[4 * y + p // 2]]
            part = pl.multiple_of(lax.rem(p, 2) * RANK, RANK)
            line = holder // Z
            place = lax.rem(y - line // XLO + Y, Y) * XLO + lax.rem(xlo + line, XLO)
            row = yrow[place, pl.ds(part, RANK)].astype(F32)
            piece = jnp.where(lax.rem(holder, Z) == z, row, 0.0).astype(BF)
            if d == 0:
                rs_recv[0] = piece
            else:
                rs_send[d - 1] = piece
                remote(rs_send.at[d - 1], rs_recv.at[d], z_s.at[0], z_r.at[0], z_peer(d)).start()

    def g_copy(d):
        return remote(gbuf.at[0, 0], gbuf.at[0, d], g_s.at[0], g_r.at[d], z_peer(d))

    def forward(d):
        for e in range(1, Y):
            remote(gbuf.at[0, d], gbuf.at[e, d], f_s.at[0], f_r.at[0], y_peer(e)).start()

    def phase_spread():
        all_recv(rs_recv.at[pl.ds(1, Z - 1)], z_r.at[0])
        total = rs_recv[0].astype(F32)
        for d in range(1, Z):
            total = total + rs_recv[d].astype(F32)
        gbuf[0, 0] = total.astype(BF)
        for d in (4, 3, 5, 2, 6, 1, 7):
            g_copy(d).start()
        forward(0)

    def phase_forward(*ds):
        for d in ds:
            g_copy(d).wait_recv()
            forward(d)

    p_copy = lambda j: remote(psend.at[j], precv.at[j], p_s.at[0], p_r.at[j], partner)
    c_copy = lambda k: remote(csend.at[k], crecv.at[k], c_s.at[0], c_r.at[0], partner)

    def x_copy(j):
        return remote(
            xsend.at[j], xrecv.at[lax.rem(j, 2), core],
            x_s.at[0], x_r.at[lax.rem(j, 2), core],
            (req, (1 - hi) * 2 + j // 2),
        )

    def project(a, base, chunk):
        return jnp.dot(
            a, w[:, pl.ds(pl.multiple_of(base, 128), chunk)], preferred_element_type=F32
        )

    mine = pl.multiple_of(core * half, half)
    other = pl.multiple_of((1 - core) * half, half)
    CH = 1280

    def pickup(j):
        p_copy(j).wait_recv()
        for n in range(0, half, CH):
            cols = pl.ds(n, CH)
            xsend[j, :, cols] = (pkeep[j, :, cols] + precv[j, :, cols].astype(F32)).astype(BF)
        x_copy(j).start()

    def request_of(step):
        there = (1 - hi) * 4 + step
        partners = hi * 4 + (1 - core) * 2 + step - 4
        own = hi * 4 + core * 2 + step - 6
        return jnp.where(step < 4, there, jnp.where(step < 6, partners, own))

    contract = (((1,), (1,)), ((), ()))

    def score(r, h, pages, count):
        cols = pl.ds(h * HD, HD)
        rows = pl.ds(pl.multiple_of(r * 128, 128), 128)
        qh = q[rows, cols]
        for g in range(0, 8, 2):
            k2 = jnp.concatenate([kp[pages[g], :, cols], kp[pages[g + 1], :, cols]], axis=0)
            s = lax.dot_general(qh, k2, contract, preferred_element_type=F32)
            sbuf[h % 2, :, pl.ds(g * 128, 256)] = s
        fresh = lax.dot_general(qh, fk[rows, cols], contract, preferred_element_type=F32)
        key_at = lax.broadcasted_iota(jnp.int32, fresh.shape, 1)
        sbuf[h % 2, :, pl.ds(1024, 128)] = jnp.where(key_at < count, fresh, NEG)

    def weigh(h):
        s = sbuf[h % 2]
        peak = jnp.max(s, axis=1, keepdims=True)
        p = jnp.exp2((s - peak) * SCALE)
        pbuf[h % 2] = p.astype(BF)
        return jnp.sum(p, axis=1, keepdims=True)

    def blend(r, h, pages, count, total):
        cols = pl.ds(h * HD, HD)
        rows = pl.ds(pl.multiple_of(r * 128, 128), 128)
        v = jnp.concatenate([vp[pages[g], :, cols] for g in range(8)] + [fv[rows, cols]], axis=0)
        o = jnp.dot(pbuf[h % 2], v, preferred_element_type=F32) / total
        slot_at = lax.broadcasted_iota(jnp.int32, o.shape, 0)
        att[r, :, cols] = jnp.where(slot_at < count, o, 0.0).astype(BF)

    for cp in early:
        cp.wait()

    events = EVENTS

    def step_body(step, carry):
        r = request_of(step)
        pages = [pt[r, g] for g in range(8)]
        count = live[r]

        def at_step(n, fn):
            pl.when(step == n)(fn)

        def run_events(gap):
            for (n, g), name in events.items():
                if g == gap:
                    at_step(n, phases[name])

        def wait_late():
            for cp in late:
                cp.wait()

        at_step(4, wait_late)

        totals = {}
        score(r, 0, pages, count)
        for h in range(heads + 1):
            if h + 1 < heads:
                score(r, h + 1, pages, count)
            if h >= 1:
                blend(r, h - 1, pages, count, totals[h - 1])
            if h < heads:
                totals[h] = weigh(h)

        pl.when((step >= 1) & (step <= 4))(lambda: pickup(step - 1))
        run_events("a")
        at_step(0, load_w.wait)
        a = att[r]

        @pl.when(step < 4)
        def _():
            psend[step] = project(a, other, half).astype(BF)
            p_copy(step).start()
            pkeep[step] = project(a, mine, half)

        @pl.when((step >= 4) & (step < 6))
        def _():
            for n in range(0, n_out, CH):
                csend[step - 4, :, pl.ds(n, CH)] = project(a, n, CH).astype(BF)
            c_copy(step - 4).start()

        @pl.when(step >= 6)
        def _():
            for n in range(0, n_out, CH):
                acc[step - 6, :, pl.ds(n, CH)] = project(a, n, CH)

        run_events("b")
        return carry

    phases = {
        "sum": phase_sum,
        "spread": phase_spread,
        "f17": lambda: phase_forward(1, 7),
        "f26": lambda: phase_forward(2, 6),
        "f35": lambda: phase_forward(3, 5),
        "f4": lambda: phase_forward(4),
    }
    lax.fori_loop(0, 8, step_body, 0)

    all_recv(gbuf.at[pl.ds(1, Y - 1)], f_r.at[0])
    ra_copy = lambda d: remote(rsend.at[d - 1], rbuf.at[d], ra_s.at[0], ra_r.at[0], tp_peer(d))
    u_copy = lambda d: remote(usend.at[d - 1], ubuf.at[d], u_s.at[0], u_r.at[0], tp_peer(d))
    for d in (2, 3, 1, 0):
        for k in range(2):
            r = lax.rem(tp + d, 4) * 2 + k
            s = slot_of[r]
            group = lax.rem(y - s // 4 + Y, Y)
            p = lax.rem(s, 4) * 2
            down = gbuf[group, lax.rem(z - p + Z, Z)]
            up = gbuf[group, lax.rem(z - p - 1 + Z, Z)]
            ranked = lax.dot_general(
                down, att[r], (((1,), (1,)), ((), ())), preferred_element_type=F32
            )
            if d == 0:
                rbuf[0, k] = ranked
                ubuf[0, k] = up
            else:
                rsend[d - 1, k] = ranked
                usend[d - 1, k] = up
        if d:
            ra_copy(d).start()
            u_copy(d).start()

    all_recv(crecv, c_r.at[0])
    all_recv(rbuf.at[pl.ds(1, 3)], ra_r.at[0])
    all_recv(ubuf.at[pl.ds(1, 3)], u_r.at[0])

    for k in range(2):
        ra = rbuf[0, k] + rbuf[1, k] + rbuf[2, k] + rbuf[3, k]
        top = ra.astype(BF)
        rest = ra - top.astype(F32)
        mid = rest.astype(BF)
        low = (rest - mid.astype(F32)).astype(BF)
        ra3 = jnp.concatenate([top, mid, low], axis=0)
        for n in range(4):
            cols = pl.ds(n * width, width)
            u1 = ubuf[lax.rem(tp - n + 4, 4), k]
            u3 = jnp.concatenate([u1, u1, u1], axis=0)
            term = lax.dot_general(ra3, u3, (((0,), (0,)), ((), ())), preferred_element_type=F32)
            acc[k, :, cols] = acc[k, :, cols] + crecv[k, :, cols].astype(F32) + term

    for k in range(2):
        for cs in range(2):
            remote(xsend.at[0], xrecv.at[k, cs], x_s.at[0], x_r.at[k, cs], partner).wait_recv()
            cols = pl.ds(cs * half, half)
            out[pl.ds(k * 128, 128), cols] = acc[k, :, cols] + xrecv[k, cs].astype(F32)

    all_sent(yrow.at[pl.ds(1, Y * XLO - 1)], y_s.at[0])
    all_sent(rs_send, z_s.at[0])
    all_sent(gbuf.at[0, pl.ds(1, Z - 1)], g_s.at[0])
    all_sent(gbuf.at[pl.ds(1, Y - 1)], f_s.at[0])
    all_sent(psend, p_s.at[0])
    all_sent(xsend, x_s.at[0])
    all_sent(csend, c_s.at[0])
    all_sent(rsend, ra_s.at[0])
    all_sent(usend, u_s.at[0])


def body(
    queries, fresh_keys, fresh_values, paged_keys, paged_values, request_page_table,
    live_token_count, request_adapter_slot, adapters_in_use, adapter_pool_row,
    adapter_down_factors, adapter_up_factors, output_weight, gating,
):
    rows, width = queries.shape
    n_out = output_weight.shape[1]
    half = n_out // 2
    hbm = pl.BlockSpec(memory_space=pltpu.HBM)
    smem = pl.BlockSpec(memory_space=pltpu.SMEM)
    V = pltpu.VMEM
    dma = pltpu.SemaphoreType.DMA
    one = dma((1,))
    def pinned(*xs):
        return [pltpu.with_memory_space_constraint(x, pltpu.HBM) for x in xs]

    total = pl.pallas_call(
        kernel,
        out_shape=jax.ShapeDtypeStruct((rows // 4, n_out), F32),
        in_specs=[hbm] * 8 + [smem] * 5,
        out_specs=pl.BlockSpec(memory_space=V),
        scratch_shapes=[
            V((rows, width), BF), V((rows, width), BF), V((rows, width), BF),
            V(paged_keys.shape, BF), V(paged_values.shape, BF), V((width, n_out), BF),
            V((2, 128, 1152), F32), V((2, 128, 1152), BF), V((8, 128, width), BF),
            V((4, 128, half), BF), V((4, 128, half), BF), V((4, 128, half), F32), V((4, 128, half), BF),
            V((2, 128, n_out), BF), V((2, 128, n_out), BF), V((2, 128, n_out), F32),
            V((2, 2, 128, half), BF),
            V((Y * XLO, 2 * RANK, width), BF), V((Z - 1, RANK, width), BF), V((Z, RANK, width), BF),
            V((Y, Z, RANK, width), BF),
            V((4, 2, RANK, 128), F32), V((4, 2, RANK, width), BF),
            V((3, 2, RANK, 128), F32), V((3, 2, RANK, width), BF),
            dma((11,)),
            one, dma((4,)), one, dma((2, 2)), one, one, one, one, one, one,
            one, dma((Z,)), one, one, one, one, one, one,
        ],
        compiler_params=pltpu.CompilerParams(
            collective_id=0, has_side_effects=True, vmem_limit_bytes=48 * 1024 * 1024
        ),
        name="attend_project",
    )(
        *pinned(
            queries, fresh_keys, fresh_values, paged_keys, paged_values,
            adapter_down_factors, adapter_up_factors, output_weight,
            request_page_table, live_token_count, request_adapter_slot, adapters_in_use, adapter_pool_row,
        )
    )
    gate = lax.dynamic_slice_in_dim(gating, lax.axis_index("tp") * 2, 2, 0)
    gated = gate[:, None, :] * total.reshape(2, -1, n_out)
    return gated.reshape(-1, n_out).astype(BF)


def solution(mesh):
    return jax.shard_map(
        body,
        mesh=mesh,
        in_specs=(
            P("req", "tp"), P("req", "tp"), P("req", "tp"),
            P("req", None, "tp"), P("req", None, "tp"),
            P("req", None), P("req"), P("req"), P(), P(),
            P("req", None, "tp"), P("req", None, None), P("tp", None), P("req", None),
        ),
        out_specs=P(("req", "tp"), None),
        check_vma=False,
    )
```

```python
import functools
import math

import jax
import jax.numpy as jnp
from jax import lax
from jax.experimental import pallas as pl
from jax.experimental.pallas import tpu as pltpu
from jax.sharding import PartitionSpec as P

HD = 128
RANK = 16
MESH = pl.DeviceIdType.MESH
NEG = -1e30
SCALE = math.log2(math.e) / math.sqrt(HD)
BF = jnp.bfloat16
F32 = jnp.float32
Y, XLO, Z = 4, 2, 8
EVENTS = {
    (1, "a"): "sum", (3, "b"): "spread",
    (5, "a"): "f17", (5, "b"): "f26", (6, "a"): "f35", (6, "b"): "f4",
}


def kernel(
    q_hbm, fk_hbm, fv_hbm, kp_hbm, vp_hbm, down_hbm, up_hbm, w_hbm,
    pt, live, slot_of, in_use, pool_row,
    out,
    q, fk, fv, kp, vp, w,
    sbuf, pbuf, att, psend, precv, pkeep, xsend, csend, crecv, acc, xrecv,
    yrow, rs_send, rs_recv, gbuf, rbuf, ubuf, rsend, usend,
    lsem,
    p_s, p_r, x_s, x_r, c_s, c_r, y_s, y_r, z_s, z_r, g_s, g_r, f_s, f_r, ra_s, ra_r, u_s, u_r,
):
    req = lax.axis_index("req")
    tp = lax.axis_index("tp")
    z = lax.rem(req, Z)
    yx = req // Z
    y = yx // XLO
    xlo = lax.rem(yx, XLO)
    hi = tp // 2
    core = lax.rem(tp, 2)
    width = q.shape[1]
    heads = width // HD
    n_out = w.shape[1]
    half = n_out // 2

    def at(y_, xlo_, z_):
        return (y_ * XLO + xlo_) * Z + z_

    partner = (req, hi * 2 + 1 - core)
    tp_peer = lambda d: (req, lax.rem(tp + d, 4))
    z_peer = lambda d: (at(y, xlo, lax.rem(z + d, Z)), tp)
    y_peer = lambda d: (at(lax.rem(y + d, Y), xlo, z), tp)

    def plane_peer(e):
        return (at(lax.rem(y + e // 2, Y), lax.rem(xlo + e, 2), z), tp)


    first = pl.multiple_of((1 - hi) * 512, 512)
    second = pl.multiple_of(hi * 512, 512)
    loads = []

    def load(src, dst):
        cp = pltpu.make_async_copy(src, dst, lsem.at[len(loads)])
        cp.start()
        loads.append(cp)
        return cp

    own_down = load(down_hbm.at[0], yrow.at[0, pl.ds(0, RANK)])
    own_up = load(
        up_hbm.at[0, :, pl.ds(pl.multiple_of(tp * width, width), width)],
        yrow.at[0, pl.ds(RANK, RANK)],
    )
    rest = pl.multiple_of(first + 128, 128)
    early = [
        load(kp_hbm, kp),
        load(q_hbm.at[pl.ds(first, 128)], q.at[pl.ds(first, 128)]),
        load(fk_hbm.at[pl.ds(first, 128)], fk.at[pl.ds(first, 128)]),
        load(vp_hbm, vp),
        load(fv_hbm.at[pl.ds(first, 128)], fv.at[pl.ds(first, 128)]),
    ]
    load_w = load(w_hbm, w)
    following = [
        load(q_hbm.at[pl.ds(rest, 384)], q.at[pl.ds(rest, 384)]),
        load(fk_hbm.at[pl.ds(rest, 384)], fk.at[pl.ds(rest, 384)]),
        load(fv_hbm.at[pl.ds(rest, 384)], fv.at[pl.ds(rest, 384)]),
    ]
    late = [
        load(q_hbm.at[pl.ds(second, 512)], q.at[pl.ds(second, 512)]),
        load(fk_hbm.at[pl.ds(second, 512)], fk.at[pl.ds(second, 512)]),
        load(fv_hbm.at[pl.ds(second, 512)], fv.at[pl.ds(second, 512)]),
    ]

    barrier = pltpu.get_barrier_semaphore()
    peers = [tp_peer(d) for d in range(1, 4)] + [z_peer(d) for d in range(1, Z)]
    peers += [plane_peer(e) for e in range(1, Y * XLO)]
    for p in peers:
        pl.semaphore_signal(barrier, inc=1, device_id=p, device_id_type=MESH)
    pl.semaphore_wait(barrier, len(peers))

    def remote(src, dst, ss, rs, dev):
        return pltpu.make_async_remote_copy(src, dst, ss, rs, device_id=dev, device_id_type=MESH)

    def all_recv(buf, rs):
        remote(buf, buf, z_s.at[0], rs, partner).wait_recv()

    def all_sent(buf, ss):
        remote(buf, buf, ss, z_r.at[0], partner).wait_send()

    own_down.wait()
    own_up.wait()
    for e in range(1, Y * XLO):
        remote(yrow.at[0], yrow.at[e], y_s.at[0], y_r.at[0], plane_peer(e)).start()

    def phase_sum():
        all_recv(yrow.at[pl.ds(1, Y * XLO - 1)], y_r.at[0])
        for d in range(Z):
            p = lax.rem(z + d, Z)
            holder = pool_row[in_use[4 * y + p // 2]]
            part = pl.multiple_of(lax.rem(p, 2) * RANK, RANK)
            line = holder // Z
            place = lax.rem(y - line // XLO + Y, Y) * XLO + lax.rem(xlo + line, XLO)
            row = yrow[place, pl.ds(part, RANK)].astype(F32)
            piece = jnp.where(lax.rem(holder, Z) == z, row, 0.0).astype(BF)
            if d == 0:
                rs_recv[0] = piece
            else:
                rs_send[d - 1] = piece
                remote(rs_send.at[d - 1], rs_recv.at[d], z_s.at[0], z_r.at[0], z_peer(d)).start()

    def g_copy(d):
        return remote(gbuf.at[0, 0], gbuf.at[0, d], g_s.at[0], g_r.at[d], z_peer(d))

    def forward(d):
        for e in range(1, Y):
            remote(gbuf.at[0, d], gbuf.at[e, d], f_s.at[0], f_r.at[0], y_peer(e)).start()

    def phase_spread():
        all_recv(rs_recv.at[pl.ds(1, Z - 1)], z_r.at[0])
        total = rs_recv[0].astype(F32)
        for d in range(1, Z):
            total = total + rs_recv[d].astype(F32)
        gbuf[0, 0] = total.astype(BF)
        for d in (4, 3, 5, 2, 6, 1, 7):
            g_copy(d).start()
        forward(0)

    def phase_forward(*ds):
        for d in ds:
            g_copy(d).wait_recv()
            forward(d)

    HALF = half // 2

    def p_copy(j, c):
        cols = pl.ds(c * HALF, HALF)
        return remote(
            psend.at[j, :, cols], precv.at[j, :, cols], p_s.at[0], p_r.at[j, c], partner
        )

    c_copy = lambda k: remote(csend.at[k], crecv.at[k], c_s.at[0], c_r.at[0], partner)

    def x_copy(j, c):
        cols = pl.ds(c * HALF, HALF)
        return remote(
            xsend.at[j, :, cols], xrecv.at[lax.rem(j, 2), core, :, cols],
            x_s.at[0], x_r.at[lax.rem(j, 2), core],
            (req, (1 - hi) * 2 + j // 2),
        )

    def project(a, base, chunk):
        return jnp.dot(
            a, w[:, pl.ds(pl.multiple_of(base, 128), chunk)], preferred_element_type=F32
        )

    mine = pl.multiple_of(core * half, half)
    other = pl.multiple_of((1 - core) * half, half)
    CH = 1280

    def pickup(j):
        for c in range(2):
            p_copy(j, c).wait_recv()
            cols = pl.ds(c * HALF, HALF)
            xsend[j, :, cols] = (pkeep[j, :, cols] + precv[j, :, cols].astype(F32)).astype(BF)
            if c == 0:
                x_copy(j, 0).start()
            else:
                pl.when(j < 3)(lambda: x_copy(j, 1).start())

    def request_of(step):
        there = (1 - hi) * 4 + step
        partners = hi * 4 + (1 - core) * 2 + step - 4
        own = hi * 4 + core * 2 + step - 6
        return jnp.where(step < 4, there, jnp.where(step < 6, partners, own))

    contract = (((1,), (1,)), ((), ()))

    def score(r, h, pages, count):
        cols = pl.ds(h * HD, HD)
        rows = pl.ds(pl.multiple_of(r * 128, 128), 128)
        qh = q[rows, cols]
        for g in range(0, 8, 2):
            k2 = jnp.concatenate([kp[pages[g], :, cols], kp[pages[g + 1], :, cols]], axis=0)
            s = lax.dot_general(qh, k2, contract, preferred_element_type=F32)
            sbuf[h % 2, :, pl.ds(g * 128, 256)] = s
        fresh = lax.dot_general(qh, fk[rows, cols], contract, preferred_element_type=F32)
        key_at = lax.broadcasted_iota(jnp.int32, fresh.shape, 1)
        sbuf[h % 2, :, pl.ds(1024, 128)] = jnp.where(key_at < count, fresh, NEG)

    def weigh(h):
        s = sbuf[h % 2]
        peak = jnp.max(s, axis=1, keepdims=True)
        p = jnp.exp2((s - peak) * SCALE)
        pbuf[h % 2] = p.astype(BF)
        return jnp.sum(p, axis=1, keepdims=True)

    def blend(r, h, pages, count, total):
        cols = pl.ds(h * HD, HD)
        rows = pl.ds(pl.multiple_of(r * 128, 128), 128)
        v = jnp.concatenate([vp[pages[g], :, cols] for g in range(8)] + [fv[rows, cols]], axis=0)
        o = jnp.dot(pbuf[h % 2], v, preferred_element_type=F32) / total
        slot_at = lax.broadcasted_iota(jnp.int32, o.shape, 0)
        att[r, :, cols] = jnp.where(slot_at < count, o, 0.0).astype(BF)

    for cp in early:
        cp.wait()

    events = EVENTS

    def step_body(step, carry):
        r = request_of(step)
        pages = [pt[r, g] for g in range(8)]
        count = live[r]

        def at_step(n, fn):
            pl.when(step == n)(fn)

        def run_events(gap):
            for (n, g), name in events.items():
                if g == gap:
                    at_step(n, phases[name])

        def wait_late():
            for cp in late:
                cp.wait()

        def wait_following():
            for cp in following:
                cp.wait()

        at_step(1, wait_following)
        at_step(4, wait_late)

        totals = {}
        score(r, 0, pages, count)
        for h in range(heads + 1):
            if h + 1 < heads:
                score(r, h + 1, pages, count)
            if h >= 1:
                blend(r, h - 1, pages, count, totals[h - 1])
            if h < heads:
                totals[h] = weigh(h)

        pl.when((step >= 2) & (step <= 4))(lambda: pickup(step - 1))
        run_events("a")
        at_step(0, load_w.wait)
        a = att[r]

        @pl.when(step < 4)
        def _():
            for c in range(2):
                psend[step, :, pl.ds(c * HALF, HALF)] = project(a, other + c * HALF, HALF).astype(BF)
                p_copy(step, c).start()
            pkeep[step] = project(a, mine, half)

        @pl.when((step >= 4) & (step < 6))
        def _():
            for n in range(0, n_out, CH):
                csend[step - 4, :, pl.ds(n, CH)] = project(a, n, CH).astype(BF)
            c_copy(step - 4).start()

        @pl.when(step >= 6)
        def _():
            for n in range(0, n_out, CH):
                acc[step - 6, :, pl.ds(n, CH)] = project(a, n, CH)

        at_step(0, lambda: pickup(0))
        run_events("b")
        return carry

    phases = {
        "sum": phase_sum,
        "spread": phase_spread,
        "f17": lambda: phase_forward(1, 7),
        "f26": lambda: phase_forward(2, 6),
        "f35": lambda: phase_forward(3, 5),
        "f4": lambda: phase_forward(4),
    }
    lax.fori_loop(0, 8, step_body, 0)

    all_recv(gbuf.at[pl.ds(1, Y - 1)], f_r.at[0])
    ra_copy = lambda d: remote(rsend.at[d - 1], rbuf.at[d], ra_s.at[0], ra_r.at[0], tp_peer(d))
    u_copy = lambda d: remote(usend.at[d - 1], ubuf.at[d], u_s.at[0], u_r.at[0], tp_peer(d))
    for d in (2, 3, 1, 0):
        for k in range(2):
            r = lax.rem(tp + d, 4) * 2 + k
            s = slot_of[r]
            group = lax.rem(y - s // 4 + Y, Y)
            p = lax.rem(s, 4) * 2
            down = gbuf[group, lax.rem(z - p + Z, Z)]
            up = gbuf[group, lax.rem(z - p - 1 + Z, Z)]
            ranked = lax.dot_general(
                down, att[r], (((1,), (1,)), ((), ())), preferred_element_type=F32
            )
            if d == 0:
                rbuf[0, k] = ranked
                ubuf[0, k] = up
            else:
                rsend[d - 1, k] = ranked
                usend[d - 1, k] = up
        if d:
            ra_copy(d).start()
            u_copy(d).start()

    x_copy(3, 1).start()
    all_recv(crecv, c_r.at[0])
    all_recv(rbuf.at[pl.ds(1, 3)], ra_r.at[0])
    all_recv(ubuf.at[pl.ds(1, 3)], u_r.at[0])

    for k in range(2):
        ra = rbuf[0, k] + rbuf[1, k] + rbuf[2, k] + rbuf[3, k]
        top = ra.astype(BF)
        rest = ra - top.astype(F32)
        mid = rest.astype(BF)
        low = (rest - mid.astype(F32)).astype(BF)
        ra3 = jnp.concatenate([top, mid, low], axis=0)
        for n in range(4):
            cols = pl.ds(n * width, width)
            u1 = ubuf[lax.rem(tp - n + 4, 4), k]
            u3 = jnp.concatenate([u1, u1, u1], axis=0)
            term = lax.dot_general(ra3, u3, (((0,), (0,)), ((), ())), preferred_element_type=F32)
            acc[k, :, cols] = acc[k, :, cols] + crecv[k, :, cols].astype(F32) + term

    for k in range(2):
        for cs in range(2):
            remote(xsend.at[0], xrecv.at[k, cs], x_s.at[0], x_r.at[k, cs], partner).wait_recv()
            cols = pl.ds(cs * half, half)
            out[pl.ds(k * 128, 128), cols] = acc[k, :, cols] + xrecv[k, cs].astype(F32)

    all_sent(yrow.at[pl.ds(1, Y * XLO - 1)], y_s.at[0])
    all_sent(rs_send, z_s.at[0])
    all_sent(gbuf.at[0, pl.ds(1, Z - 1)], g_s.at[0])
    all_sent(gbuf.at[pl.ds(1, Y - 1)], f_s.at[0])
    all_sent(psend, p_s.at[0])
    all_sent(xsend, x_s.at[0])
    all_sent(csend, c_s.at[0])
    all_sent(rsend, ra_s.at[0])
    all_sent(usend, u_s.at[0])


def body(
    queries, fresh_keys, fresh_values, paged_keys, paged_values, request_page_table,
    live_token_count, request_adapter_slot, adapters_in_use, adapter_pool_row,
    adapter_down_factors, adapter_up_factors, output_weight, gating,
):
    rows, width = queries.shape
    n_out = output_weight.shape[1]
    half = n_out // 2
    hbm = pl.BlockSpec(memory_space=pltpu.HBM)
    smem = pl.BlockSpec(memory_space=pltpu.SMEM)
    V = pltpu.VMEM
    dma = pltpu.SemaphoreType.DMA
    one = dma((1,))
    def pinned(*xs):
        return [pltpu.with_memory_space_constraint(x, pltpu.HBM) for x in xs]

    total = pl.pallas_call(
        kernel,
        out_shape=jax.ShapeDtypeStruct((rows // 4, n_out), F32),
        in_specs=[hbm] * 8 + [smem] * 5,
        out_specs=pl.BlockSpec(memory_space=V),
        scratch_shapes=[
            V((rows, width), BF), V((rows, width), BF), V((rows, width), BF),
            V(paged_keys.shape, BF), V(paged_values.shape, BF), V((width, n_out), BF),
            V((2, 128, 1152), F32), V((2, 128, 1152), BF), V((8, 128, width), BF),
            V((4, 128, half), BF), V((4, 128, half), BF), V((4, 128, half), F32), V((4, 128, half), BF),
            V((2, 128, n_out), BF), V((2, 128, n_out), BF), V((2, 128, n_out), F32),
            V((2, 2, 128, half), BF),
            V((Y * XLO, 2 * RANK, width), BF), V((Z - 1, RANK, width), BF), V((Z, RANK, width), BF),
            V((Y, Z, RANK, width), BF),
            V((4, 2, RANK, 128), F32), V((4, 2, RANK, width), BF),
            V((3, 2, RANK, 128), F32), V((3, 2, RANK, width), BF),
            dma((14,)),
            one, dma((4, 2)), one, dma((2, 2)), one, one, one, one, one, one,
            one, dma((Z,)), one, one, one, one, one, one,
        ],
        compiler_params=pltpu.CompilerParams(
            collective_id=0, has_side_effects=True, vmem_limit_bytes=48 * 1024 * 1024
        ),
        name="attend_project",
    )(
        *pinned(
            queries, fresh_keys, fresh_values, paged_keys, paged_values,
            adapter_down_factors, adapter_up_factors, output_weight,
            request_page_table, live_token_count, request_adapter_slot, adapters_in_use, adapter_pool_row,
        )
    )
    gate = lax.dynamic_slice_in_dim(gating, lax.axis_index("tp") * 2, 2, 0)
    gated = gate[:, None, :] * total.reshape(2, -1, n_out)
    return gated.reshape(-1, n_out).astype(BF)


def solution(mesh):
    return jax.shard_map(
        body,
        mesh=mesh,
        in_specs=(
            P("req", "tp"), P("req", "tp"), P("req", "tp"),
            P("req", None, "tp"), P("req", None, "tp"),
            P("req", None), P("req"), P("req"), P(), P(),
            P("req", None, "tp"), P("req", None, None), P("tp", None), P("req", None),
        ),
        out_specs=P(("req", "tp"), None),
        check_vma=False,
    )
```

```python
import functools
import math

import jax
import jax.numpy as jnp
from jax import lax
from jax.experimental import pallas as pl
from jax.experimental.pallas import tpu as pltpu
from jax.sharding import PartitionSpec as P

HD = 128
RANK = 16
MESH = pl.DeviceIdType.MESH
NEG = -1e30
SCALE = math.log2(math.e) / math.sqrt(HD)
BF = jnp.bfloat16
F32 = jnp.float32
Y, XLO, Z = 4, 2, 8
EVENTS = {
    (1, "a"): "sum", (3, "b"): "spread",
    (5, "a"): "f17", (5, "b"): "f26", (6, "a"): "f35", (6, "b"): "f4",
}


def kernel(
    q_hbm, fk_hbm, fv_hbm, kp_hbm, vp_hbm, down_hbm, up_hbm, w_hbm,
    pt, live, slot_of, in_use, pool_row,
    out,
    q, fk, fv, kp, vp, w,
    sbuf, pbuf, att, psend, precv, pkeep, xsend, csend, crecv, acc, xrecv,
    yrow, rs_send, rs_recv, gbuf, rbuf, ubuf, rsend, usend,
    lsem,
    p_s, p_r, x_s, x_r, c_s, c_r, y_s, y_r, z_s, z_r, g_s, g_r, f_s, f_r, ra_s, ra_r, u_s, u_r,
):
    req = lax.axis_index("req")
    tp = lax.axis_index("tp")
    z = lax.rem(req, Z)
    yx = req // Z
    y = yx // XLO
    xlo = lax.rem(yx, XLO)
    hi = tp // 2
    core = lax.rem(tp, 2)
    width = q.shape[1]
    heads = width // HD
    n_out = w.shape[1]
    half = n_out // 2

    def at(y_, xlo_, z_):
        return (y_ * XLO + xlo_) * Z + z_

    partner = (req, hi * 2 + 1 - core)
    tp_peer = lambda d: (req, lax.rem(tp + d, 4))
    z_peer = lambda d: (at(y, xlo, lax.rem(z + d, Z)), tp)
    y_peer = lambda d: (at(lax.rem(y + d, Y), xlo, z), tp)

    def plane_peer(e):
        return (at(lax.rem(y + e // 2, Y), lax.rem(xlo + e, 2), z), tp)


    first = pl.multiple_of((1 - hi) * 512, 512)
    second = pl.multiple_of(hi * 512, 512)
    loads = []

    def load(src, dst):
        cp = pltpu.make_async_copy(src, dst, lsem.at[len(loads)])
        cp.start()
        loads.append(cp)
        return cp

    own_down = load(down_hbm.at[0], yrow.at[0, pl.ds(0, RANK)])
    own_up = load(
        up_hbm.at[0, :, pl.ds(pl.multiple_of(tp * width, width), width)],
        yrow.at[0, pl.ds(RANK, RANK)],
    )
    rest = pl.multiple_of(first + 128, 128)
    early = [
        load(kp_hbm, kp),
        load(q_hbm.at[pl.ds(first, 128)], q.at[pl.ds(first, 128)]),
        load(fk_hbm.at[pl.ds(first, 128)], fk.at[pl.ds(first, 128)]),
        load(vp_hbm, vp),
        load(fv_hbm.at[pl.ds(first, 128)], fv.at[pl.ds(first, 128)]),
    ]
    load_w = load(w_hbm, w)
    following = [
        load(q_hbm.at[pl.ds(rest, 384)], q.at[pl.ds(rest, 384)]),
        load(fk_hbm.at[pl.ds(rest, 384)], fk.at[pl.ds(rest, 384)]),
        load(fv_hbm.at[pl.ds(rest, 384)], fv.at[pl.ds(rest, 384)]),
    ]
    late = [
        load(q_hbm.at[pl.ds(second, 512)], q.at[pl.ds(second, 512)]),
        load(fk_hbm.at[pl.ds(second, 512)], fk.at[pl.ds(second, 512)]),
        load(fv_hbm.at[pl.ds(second, 512)], fv.at[pl.ds(second, 512)]),
    ]

    barrier = pltpu.get_barrier_semaphore()
    peers = [tp_peer(d) for d in range(1, 4)] + [z_peer(d) for d in range(1, Z)]
    peers += [plane_peer(e) for e in range(1, Y * XLO)]
    for p in peers:
        pl.semaphore_signal(barrier, inc=1, device_id=p, device_id_type=MESH)

    def remote(src, dst, ss, rs, dev):
        return pltpu.make_async_remote_copy(src, dst, ss, rs, device_id=dev, device_id_type=MESH)

    def all_recv(buf, rs):
        remote(buf, buf, z_s.at[0], rs, partner).wait_recv()

    def all_sent(buf, ss):
        remote(buf, buf, ss, z_r.at[0], partner).wait_send()

    def phase_sum():
        all_recv(yrow.at[pl.ds(1, Y * XLO - 1)], y_r.at[0])
        for d in range(Z):
            p = lax.rem(z + d, Z)
            holder = pool_row[in_use[4 * y + p // 2]]
            part = pl.multiple_of(lax.rem(p, 2) * RANK, RANK)
            line = holder // Z
            place = lax.rem(y - line // XLO + Y, Y) * XLO + lax.rem(xlo + line, XLO)
            row = yrow[place, pl.ds(part, RANK)].astype(F32)
            piece = jnp.where(lax.rem(holder, Z) == z, row, 0.0).astype(BF)
            if d == 0:
                rs_recv[0] = piece
            else:
                rs_send[d - 1] = piece
                remote(rs_send.at[d - 1], rs_recv.at[d], z_s.at[0], z_r.at[0], z_peer(d)).start()

    def g_copy(d):
        return remote(gbuf.at[0, 0], gbuf.at[0, d], g_s.at[0], g_r.at[d], z_peer(d))

    def forward(d):
        for e in range(1, Y):
            remote(gbuf.at[0, d], gbuf.at[e, d], f_s.at[0], f_r.at[0], y_peer(e)).start()

    def phase_spread():
        all_recv(rs_recv.at[pl.ds(1, Z - 1)], z_r.at[0])
        total = rs_recv[0].astype(F32)
        for d in range(1, Z):
            total = total + rs_recv[d].astype(F32)
        gbuf[0, 0] = total.astype(BF)
        for d in (4, 3, 5, 2, 6, 1, 7):
            g_copy(d).start()
        forward(0)

    def phase_forward(*ds):
        for d in ds:
            g_copy(d).wait_recv()
            forward(d)

    HALF = half // 2

    def p_copy(j, c):
        cols = pl.ds(c * HALF, HALF)
        return remote(
            psend.at[j, :, cols], precv.at[j, :, cols], p_s.at[0], p_r.at[j, c], partner
        )

    c_copy = lambda k: remote(csend.at[k], crecv.at[k], c_s.at[0], c_r.at[0], partner)

    def x_copy(j, c):
        cols = pl.ds(c * HALF, HALF)
        return remote(
            xsend.at[j, :, cols], xrecv.at[lax.rem(j, 2), core, :, cols],
            x_s.at[0], x_r.at[lax.rem(j, 2), core],
            (req, (1 - hi) * 2 + j // 2),
        )

    def project(a, base, chunk):
        return jnp.dot(
            a, w[:, pl.ds(pl.multiple_of(base, 128), chunk)], preferred_element_type=F32
        )

    mine = pl.multiple_of(core * half, half)
    other = pl.multiple_of((1 - core) * half, half)
    CH = 1280

    def pickup(j):
        for c in range(2):
            p_copy(j, c).wait_recv()
            cols = pl.ds(c * HALF, HALF)
            xsend[j, :, cols] = (pkeep[j, :, cols] + precv[j, :, cols].astype(F32)).astype(BF)
            if c == 0:
                x_copy(j, 0).start()
            else:
                pl.when(j < 3)(lambda: x_copy(j, 1).start())

    def request_of(step):
        there = (1 - hi) * 4 + step
        partners = hi * 4 + (1 - core) * 2 + step - 4
        own = hi * 4 + core * 2 + step - 6
        return jnp.where(step < 4, there, jnp.where(step < 6, partners, own))

    contract = (((1,), (1,)), ((), ()))

    def score(r, h, pages, count):
        cols = pl.ds(h * HD, HD)
        rows = pl.ds(pl.multiple_of(r * 128, 128), 128)
        qh = q[rows, cols]
        for g in range(0, 8, 2):
            k2 = jnp.concatenate([kp[pages[g], :, cols], kp[pages[g + 1], :, cols]], axis=0)
            s = lax.dot_general(qh, k2, contract, preferred_element_type=F32)
            sbuf[h % 2, :, pl.ds(g * 128, 256)] = s
        fresh = lax.dot_general(qh, fk[rows, cols], contract, preferred_element_type=F32)
        key_at = lax.broadcasted_iota(jnp.int32, fresh.shape, 1)
        sbuf[h % 2, :, pl.ds(1024, 128)] = jnp.where(key_at < count, fresh, NEG)

    def weigh(h):
        s = sbuf[h % 2]
        peak = jnp.max(s, axis=1, keepdims=True)
        p = jnp.exp2((s - peak) * SCALE)
        pbuf[h % 2] = p.astype(BF)
        return jnp.sum(p, axis=1, keepdims=True)

    def blend(r, h, pages, count, total):
        cols = pl.ds(h * HD, HD)
        rows = pl.ds(pl.multiple_of(r * 128, 128), 128)
        v = jnp.concatenate([vp[pages[g], :, cols] for g in range(8)] + [fv[rows, cols]], axis=0)
        o = jnp.dot(pbuf[h % 2], v, preferred_element_type=F32) / total
        slot_at = lax.broadcasted_iota(jnp.int32, o.shape, 0)
        att[r, :, cols] = jnp.where(slot_at < count, o, 0.0).astype(BF)

    def attend(r, between=None):
        pages = [pt[r, g] for g in range(8)]
        count = live[r]
        totals = {}
        score(r, 0, pages, count)
        for h in range(heads + 1):
            if h + 1 < heads:
                score(r, h + 1, pages, count)
            if h >= 1:
                if h == 1 and between:
                    between()
                blend(r, h - 1, pages, count, totals[h - 1])
            if h < heads:
                totals[h] = weigh(h)

    def wait_values():
        for cp in early[3:]:
            cp.wait()

    for cp in early[:3]:
        cp.wait()
    attend((1 - hi) * 4, wait_values)

    pl.semaphore_wait(barrier, len(peers))
    own_down.wait()
    own_up.wait()
    for e in range(1, Y * XLO):
        remote(yrow.at[0], yrow.at[e], y_s.at[0], y_r.at[0], plane_peer(e)).start()

    events = EVENTS

    def step_body(step, carry):
        r = request_of(step)

        def at_step(n, fn):
            pl.when(step == n)(fn)

        def run_events(gap):
            for (n, g), name in events.items():
                if g == gap:
                    at_step(n, phases[name])

        def wait_late():
            for cp in late:
                cp.wait()

        def wait_following():
            for cp in following:
                cp.wait()

        at_step(1, wait_following)
        at_step(4, wait_late)

        pl.when(step > 0)(lambda: attend(r))
        pl.when((step >= 2) & (step <= 4))(lambda: pickup(step - 1))
        run_events("a")
        at_step(0, load_w.wait)
        a = att[r]

        @pl.when(step < 4)
        def _():
            for c in range(2):
                psend[step, :, pl.ds(c * HALF, HALF)] = project(a, other + c * HALF, HALF).astype(BF)
                p_copy(step, c).start()
            pkeep[step] = project(a, mine, half)

        @pl.when((step >= 4) & (step < 6))
        def _():
            for n in range(0, n_out, CH):
                csend[step - 4, :, pl.ds(n, CH)] = project(a, n, CH).astype(BF)
            c_copy(step - 4).start()

        @pl.when(step >= 6)
        def _():
            for n in range(0, n_out, CH):
                acc[step - 6, :, pl.ds(n, CH)] = project(a, n, CH)

        at_step(0, lambda: pickup(0))
        run_events("b")
        return carry

    phases = {
        "sum": phase_sum,
        "spread": phase_spread,
        "f17": lambda: phase_forward(1, 7),
        "f26": lambda: phase_forward(2, 6),
        "f35": lambda: phase_forward(3, 5),
        "f4": lambda: phase_forward(4),
    }
    lax.fori_loop(0, 8, step_body, 0)

    all_recv(gbuf.at[pl.ds(1, Y - 1)], f_r.at[0])
    ra_copy = lambda d: remote(rsend.at[d - 1], rbuf.at[d], ra_s.at[0], ra_r.at[0], tp_peer(d))
    u_copy = lambda d: remote(usend.at[d - 1], ubuf.at[d], u_s.at[0], u_r.at[0], tp_peer(d))
    for d in (2, 3, 1, 0):
        for k in range(2):
            r = lax.rem(tp + d, 4) * 2 + k
            s = slot_of[r]
            group = lax.rem(y - s // 4 + Y, Y)
            p = lax.rem(s, 4) * 2
            down = gbuf[group, lax.rem(z - p + Z, Z)]
            up = gbuf[group, lax.rem(z - p - 1 + Z, Z)]
            ranked = lax.dot_general(
                down, att[r], (((1,), (1,)), ((), ())), preferred_element_type=F32
            )
            if d == 0:
                rbuf[0, k] = ranked
                ubuf[0, k] = up
            else:
                rsend[d - 1, k] = ranked
                usend[d - 1, k] = up
        if d:
            ra_copy(d).start()
            u_copy(d).start()

    x_copy(3, 1).start()
    all_recv(crecv, c_r.at[0])
    all_recv(rbuf.at[pl.ds(1, 3)], ra_r.at[0])
    all_recv(ubuf.at[pl.ds(1, 3)], u_r.at[0])

    for k in range(2):
        ra = rbuf[0, k] + rbuf[1, k] + rbuf[2, k] + rbuf[3, k]
        top = ra.astype(BF)
        rest = ra - top.astype(F32)
        mid = rest.astype(BF)
        low = (rest - mid.astype(F32)).astype(BF)
        ra3 = jnp.concatenate([top, mid, low], axis=0)
        for n in range(4):
            cols = pl.ds(n * width, width)
            u1 = ubuf[lax.rem(tp - n + 4, 4), k]
            u3 = jnp.concatenate([u1, u1, u1], axis=0)
            term = lax.dot_general(ra3, u3, (((0,), (0,)), ((), ())), preferred_element_type=F32)
            acc[k, :, cols] = acc[k, :, cols] + crecv[k, :, cols].astype(F32) + term

    for k in range(2):
        for cs in range(2):
            remote(xsend.at[0], xrecv.at[k, cs], x_s.at[0], x_r.at[k, cs], partner).wait_recv()
            cols = pl.ds(cs * half, half)
            out[pl.ds(k * 128, 128), cols] = acc[k, :, cols] + xrecv[k, cs].astype(F32)

    all_sent(yrow.at[pl.ds(1, Y * XLO - 1)], y_s.at[0])
    all_sent(rs_send, z_s.at[0])
    all_sent(gbuf.at[0, pl.ds(1, Z - 1)], g_s.at[0])
    all_sent(gbuf.at[pl.ds(1, Y - 1)], f_s.at[0])
    all_sent(psend, p_s.at[0])
    all_sent(xsend, x_s.at[0])
    all_sent(csend, c_s.at[0])
    all_sent(rsend, ra_s.at[0])
    all_sent(usend, u_s.at[0])


def body(
    queries, fresh_keys, fresh_values, paged_keys, paged_values, request_page_table,
    live_token_count, request_adapter_slot, adapters_in_use, adapter_pool_row,
    adapter_down_factors, adapter_up_factors, output_weight, gating,
):
    rows, width = queries.shape
    n_out = output_weight.shape[1]
    half = n_out // 2
    hbm = pl.BlockSpec(memory_space=pltpu.HBM)
    smem = pl.BlockSpec(memory_space=pltpu.SMEM)
    V = pltpu.VMEM
    dma = pltpu.SemaphoreType.DMA
    one = dma((1,))
    def pinned(*xs):
        return [pltpu.with_memory_space_constraint(x, pltpu.HBM) for x in xs]

    total = pl.pallas_call(
        kernel,
        out_shape=jax.ShapeDtypeStruct((rows // 4, n_out), F32),
        in_specs=[hbm] * 8 + [smem] * 5,
        out_specs=pl.BlockSpec(memory_space=V),
        scratch_shapes=[
            V((rows, width), BF), V((rows, width), BF), V((rows, width), BF),
            V(paged_keys.shape, BF), V(paged_values.shape, BF), V((width, n_out), BF),
            V((2, 128, 1152), F32), V((2, 128, 1152), BF), V((8, 128, width), BF),
            V((4, 128, half), BF), V((4, 128, half), BF), V((4, 128, half), F32), V((4, 128, half), BF),
            V((2, 128, n_out), BF), V((2, 128, n_out), BF), V((2, 128, n_out), F32),
            V((2, 2, 128, half), BF),
            V((Y * XLO, 2 * RANK, width), BF), V((Z - 1, RANK, width), BF), V((Z, RANK, width), BF),
            V((Y, Z, RANK, width), BF),
            V((4, 2, RANK, 128), F32), V((4, 2, RANK, width), BF),
            V((3, 2, RANK, 128), F32), V((3, 2, RANK, width), BF),
            dma((14,)),
            one, dma((4, 2)), one, dma((2, 2)), one, one, one, one, one, one,
            one, dma((Z,)), one, one, one, one, one, one,
        ],
        compiler_params=pltpu.CompilerParams(
            collective_id=0, has_side_effects=True, vmem_limit_bytes=48 * 1024 * 1024
        ),
        name="attend_project",
    )(
        *pinned(
            queries, fresh_keys, fresh_values, paged_keys, paged_values,
            adapter_down_factors, adapter_up_factors, output_weight,
            request_page_table, live_token_count, request_adapter_slot, adapters_in_use, adapter_pool_row,
        )
    )
    gate = lax.dynamic_slice_in_dim(gating, lax.axis_index("tp") * 2, 2, 0)
    gated = gate[:, None, :] * total.reshape(2, -1, n_out)
    return gated.reshape(-1, n_out).astype(BF)


def solution(mesh):
    return jax.shard_map(
        body,
        mesh=mesh,
        in_specs=(
            P("req", "tp"), P("req", "tp"), P("req", "tp"),
            P("req", None, "tp"), P("req", None, "tp"),
            P("req", None), P("req"), P("req"), P(), P(),
            P("req", None, "tp"), P("req", None, None), P("tp", None), P("req", None),
        ),
        out_specs=P(("req", "tp"), None),
        check_vma=False,
    )
```

```python
import functools
import math

import jax
import jax.numpy as jnp
from jax import lax
from jax.experimental import pallas as pl
from jax.experimental.pallas import tpu as pltpu
from jax.sharding import PartitionSpec as P

HD = 128
RANK = 16
MESH = pl.DeviceIdType.MESH
NEG = -1e30
SCALE = math.log2(math.e) / math.sqrt(HD)
BF = jnp.bfloat16
F32 = jnp.float32
Y, XLO, Z = 4, 2, 8
EVENTS = {
    (1, "a"): "sum", (3, "b"): "spread",
    (5, "a"): "f17", (5, "b"): "f26", (6, "a"): "f35", (6, "b"): "f4",
}


def kernel(
    q_hbm, fk_hbm, fv_hbm, kp_hbm, vp_hbm, down_hbm, up_hbm, w_hbm,
    pt, live, slot_of, in_use, pool_row,
    out,
    q, fk, fv, kp, vp, w,
    sbuf, pbuf, att, psend, precv, pkeep, xsend, csend, crecv, acc, xrecv,
    yrow, rs_send, rs_recv, gbuf, rbuf, ubuf, rsend, usend,
    lsem,
    p_s, p_r, x_s, x_r, c_s, c_r, y_s, y_r, z_s, z_r, g_s, g_r, f_s, f_r, ra_s, ra_r, u_s, u_r,
):
    req = lax.axis_index("req")
    tp = lax.axis_index("tp")
    z = lax.rem(req, Z)
    yx = req // Z
    y = yx // XLO
    xlo = lax.rem(yx, XLO)
    hi = tp // 2
    core = lax.rem(tp, 2)
    width = q.shape[1]
    heads = width // HD
    n_out = w.shape[1]
    half = n_out // 2

    def at(y_, xlo_, z_):
        return (y_ * XLO + xlo_) * Z + z_

    partner = (req, hi * 2 + 1 - core)
    tp_peer = lambda d: (req, lax.rem(tp + d, 4))
    z_peer = lambda d: (at(y, xlo, lax.rem(z + d, Z)), tp)
    y_peer = lambda d: (at(lax.rem(y + d, Y), xlo, z), tp)

    def plane_peer(e):
        return (at(lax.rem(y + e // 2, Y), lax.rem(xlo + e, 2), z), tp)


    first = pl.multiple_of((1 - hi) * 512, 512)
    second = pl.multiple_of(hi * 512, 512)
    loads = []

    def load(src, dst):
        cp = pltpu.make_async_copy(src, dst, lsem.at[len(loads)])
        cp.start()
        loads.append(cp)
        return cp

    own_down = load(down_hbm.at[0], yrow.at[0, pl.ds(0, RANK)])
    own_up = load(
        up_hbm.at[0, :, pl.ds(pl.multiple_of(tp * width, width), width)],
        yrow.at[0, pl.ds(RANK, RANK)],
    )
    rest = pl.multiple_of(first + 128, 128)
    early = [
        load(kp_hbm, kp),
        load(q_hbm.at[pl.ds(first, 128)], q.at[pl.ds(first, 128)]),
        load(fk_hbm.at[pl.ds(first, 128)], fk.at[pl.ds(first, 128)]),
        load(vp_hbm, vp),
        load(fv_hbm.at[pl.ds(first, 128)], fv.at[pl.ds(first, 128)]),
    ]
    mine = pl.multiple_of(core * half, half)
    other = pl.multiple_of((1 - core) * half, half)
    load_w = load(w_hbm.at[:, pl.ds(other, half)], w.at[:, pl.ds(other, half)])
    load_w_mine = load(w_hbm.at[:, pl.ds(mine, half)], w.at[:, pl.ds(mine, half)])
    following = [
        load(q_hbm.at[pl.ds(rest, 384)], q.at[pl.ds(rest, 384)]),
        load(fk_hbm.at[pl.ds(rest, 384)], fk.at[pl.ds(rest, 384)]),
        load(fv_hbm.at[pl.ds(rest, 384)], fv.at[pl.ds(rest, 384)]),
    ]
    late = [
        load(q_hbm.at[pl.ds(second, 512)], q.at[pl.ds(second, 512)]),
        load(fk_hbm.at[pl.ds(second, 512)], fk.at[pl.ds(second, 512)]),
        load(fv_hbm.at[pl.ds(second, 512)], fv.at[pl.ds(second, 512)]),
    ]

    barrier = pltpu.get_barrier_semaphore()
    peers = [tp_peer(d) for d in range(1, 4)] + [z_peer(d) for d in range(1, Z)]
    peers += [plane_peer(e) for e in range(1, Y * XLO)]
    for p in peers:
        pl.semaphore_signal(barrier, inc=1, device_id=p, device_id_type=MESH)

    def remote(src, dst, ss, rs, dev):
        return pltpu.make_async_remote_copy(src, dst, ss, rs, device_id=dev, device_id_type=MESH)

    def all_recv(buf, rs):
        remote(buf, buf, z_s.at[0], rs, partner).wait_recv()

    def all_sent(buf, ss):
        remote(buf, buf, ss, z_r.at[0], partner).wait_send()

    def phase_sum():
        all_recv(yrow.at[pl.ds(1, Y * XLO - 1)], y_r.at[0])
        for d in range(Z):
            p = lax.rem(z + d, Z)
            holder = pool_row[in_use[4 * y + p // 2]]
            part = pl.multiple_of(lax.rem(p, 2) * RANK, RANK)
            line = holder // Z
            place = lax.rem(y - line // XLO + Y, Y) * XLO + lax.rem(xlo + line, XLO)
            row = yrow[place, pl.ds(part, RANK)].astype(F32)
            piece = jnp.where(lax.rem(holder, Z) == z, row, 0.0).astype(BF)
            if d == 0:
                rs_recv[0] = piece
            else:
                rs_send[d - 1] = piece
                remote(rs_send.at[d - 1], rs_recv.at[d], z_s.at[0], z_r.at[0], z_peer(d)).start()

    def g_copy(d):
        return remote(gbuf.at[0, 0], gbuf.at[0, d], g_s.at[0], g_r.at[d], z_peer(d))

    def forward(d):
        for e in range(1, Y):
            remote(gbuf.at[0, d], gbuf.at[e, d], f_s.at[0], f_r.at[0], y_peer(e)).start()

    def phase_spread():
        all_recv(rs_recv.at[pl.ds(1, Z - 1)], z_r.at[0])
        total = rs_recv[0].astype(F32)
        for d in range(1, Z):
            total = total + rs_recv[d].astype(F32)
        gbuf[0, 0] = total.astype(BF)
        for d in (4, 3, 5, 2, 6, 1, 7):
            g_copy(d).start()
        forward(0)

    def phase_forward(*ds):
        for d in ds:
            g_copy(d).wait_recv()
            forward(d)

    HALF = half // 2

    def p_copy(j, c):
        cols = pl.ds(c * HALF, HALF)
        return remote(
            psend.at[j, :, cols], precv.at[j, :, cols], p_s.at[0], p_r.at[j, c], partner
        )

    c_copy = lambda k: remote(csend.at[k], crecv.at[k], c_s.at[0], c_r.at[0], partner)

    def x_copy(j, c):
        cols = pl.ds(c * HALF, HALF)
        return remote(
            xsend.at[j, :, cols], xrecv.at[lax.rem(j, 2), core, :, cols],
            x_s.at[0], x_r.at[lax.rem(j, 2), core],
            (req, (1 - hi) * 2 + j // 2),
        )

    def project(a, base, chunk):
        return jnp.dot(
            a, w[:, pl.ds(pl.multiple_of(base, 128), chunk)], preferred_element_type=F32
        )

    CH = 1280

    def pickup(j):
        for c in range(2):
            p_copy(j, c).wait_recv()
            cols = pl.ds(c * HALF, HALF)
            xsend[j, :, cols] = (pkeep[j, :, cols] + precv[j, :, cols].astype(F32)).astype(BF)
            if c == 0:
                x_copy(j, 0).start()
            else:
                pl.when(j < 3)(lambda: x_copy(j, 1).start())

    def request_of(step):
        there = (1 - hi) * 4 + step
        partners = hi * 4 + (1 - core) * 2 + step - 4
        own = hi * 4 + core * 2 + step - 6
        return jnp.where(step < 4, there, jnp.where(step < 6, partners, own))

    contract = (((1,), (1,)), ((), ()))

    def score(r, h, pages, count):
        cols = pl.ds(h * HD, HD)
        rows = pl.ds(pl.multiple_of(r * 128, 128), 128)
        qh = q[rows, cols]
        for g in range(0, 8, 2):
            k2 = jnp.concatenate([kp[pages[g], :, cols], kp[pages[g + 1], :, cols]], axis=0)
            s = lax.dot_general(qh, k2, contract, preferred_element_type=F32)
            sbuf[h % 2, :, pl.ds(g * 128, 256)] = s
        fresh = lax.dot_general(qh, fk[rows, cols], contract, preferred_element_type=F32)
        key_at = lax.broadcasted_iota(jnp.int32, fresh.shape, 1)
        sbuf[h % 2, :, pl.ds(1024, 128)] = jnp.where(key_at < count, fresh, NEG)

    def weigh(h):
        s = sbuf[h % 2]
        peak = jnp.max(s, axis=1, keepdims=True)
        p = jnp.exp2((s - peak) * SCALE)
        pbuf[h % 2] = p.astype(BF)
        return jnp.sum(p, axis=1, keepdims=True)

    def blend(r, h, pages, count, total):
        cols = pl.ds(h * HD, HD)
        rows = pl.ds(pl.multiple_of(r * 128, 128), 128)
        v = jnp.concatenate([vp[pages[g], :, cols] for g in range(8)] + [fv[rows, cols]], axis=0)
        o = jnp.dot(pbuf[h % 2], v, preferred_element_type=F32) / total
        slot_at = lax.broadcasted_iota(jnp.int32, o.shape, 0)
        att[r, :, cols] = jnp.where(slot_at < count, o, 0.0).astype(BF)

    def attend(r, between=None):
        pages = [pt[r, g] for g in range(8)]
        count = live[r]
        totals = {}
        score(r, 0, pages, count)
        for h in range(heads + 1):
            if h + 1 < heads:
                score(r, h + 1, pages, count)
            if h >= 1:
                if h == 1 and between:
                    between()
                blend(r, h - 1, pages, count, totals[h - 1])
            if h < heads:
                totals[h] = weigh(h)

    def wait_values():
        for cp in early[3:]:
            cp.wait()

    for cp in early[:3]:
        cp.wait()
    attend((1 - hi) * 4, wait_values)

    pl.semaphore_wait(barrier, len(peers))
    own_down.wait()
    own_up.wait()
    for e in range(1, Y * XLO):
        remote(yrow.at[0], yrow.at[e], y_s.at[0], y_r.at[0], plane_peer(e)).start()

    events = EVENTS

    def step_body(step, carry):
        r = request_of(step)

        def at_step(n, fn):
            pl.when(step == n)(fn)

        def run_events(gap):
            for (n, g), name in events.items():
                if g == gap:
                    at_step(n, phases[name])

        def wait_late():
            for cp in late:
                cp.wait()

        def wait_following():
            for cp in following:
                cp.wait()

        at_step(1, wait_following)
        at_step(4, wait_late)

        pl.when(step > 0)(lambda: attend(r))
        pl.when((step >= 2) & (step <= 4))(lambda: pickup(step - 1))
        run_events("a")
        at_step(0, load_w.wait)
        a = att[r]

        @pl.when(step < 4)
        def _():
            for c in range(2):
                psend[step, :, pl.ds(c * HALF, HALF)] = project(a, other + c * HALF, HALF).astype(BF)
                p_copy(step, c).start()
            at_step(0, load_w_mine.wait)
            pkeep[step] = project(a, mine, half)

        @pl.when((step >= 4) & (step < 6))
        def _():
            for n in range(0, n_out, CH):
                csend[step - 4, :, pl.ds(n, CH)] = project(a, n, CH).astype(BF)
            c_copy(step - 4).start()

        @pl.when(step >= 6)
        def _():
            for n in range(0, n_out, CH):
                acc[step - 6, :, pl.ds(n, CH)] = project(a, n, CH)

        at_step(0, lambda: pickup(0))
        run_events("b")
        return carry

    phases = {
        "sum": phase_sum,
        "spread": phase_spread,
        "f17": lambda: phase_forward(1, 7),
        "f26": lambda: phase_forward(2, 6),
        "f35": lambda: phase_forward(3, 5),
        "f4": lambda: phase_forward(4),
    }
    lax.fori_loop(0, 8, step_body, 0)

    all_recv(gbuf.at[pl.ds(1, Y - 1)], f_r.at[0])
    ra_copy = lambda d: remote(rsend.at[d - 1], rbuf.at[d], ra_s.at[0], ra_r.at[0], tp_peer(d))
    u_copy = lambda d: remote(usend.at[d - 1], ubuf.at[d], u_s.at[0], u_r.at[0], tp_peer(d))
    for d in (2, 3, 1, 0):
        for k in range(2):
            r = lax.rem(tp + d, 4) * 2 + k
            s = slot_of[r]
            group = lax.rem(y - s // 4 + Y, Y)
            p = lax.rem(s, 4) * 2
            down = gbuf[group, lax.rem(z - p + Z, Z)]
            up = gbuf[group, lax.rem(z - p - 1 + Z, Z)]
            ranked = lax.dot_general(
                down, att[r], (((1,), (1,)), ((), ())), preferred_element_type=F32
            )
            if d == 0:
                rbuf[0, k] = ranked
                ubuf[0, k] = up
            else:
                rsend[d - 1, k] = ranked
                usend[d - 1, k] = up
        if d:
            ra_copy(d).start()
            u_copy(d).start()

    x_copy(3, 1).start()
    all_recv(crecv, c_r.at[0])
    all_recv(rbuf.at[pl.ds(1, 3)], ra_r.at[0])
    all_recv(ubuf.at[pl.ds(1, 3)], u_r.at[0])

    for k in range(2):
        ra = rbuf[0, k] + rbuf[1, k] + rbuf[2, k] + rbuf[3, k]
        top = ra.astype(BF)
        rest = ra - top.astype(F32)
        mid = rest.astype(BF)
        low = (rest - mid.astype(F32)).astype(BF)
        ra3 = jnp.concatenate([top, mid, low], axis=0)
        for n in range(4):
            cols = pl.ds(n * width, width)
            u1 = ubuf[lax.rem(tp - n + 4, 4), k]
            u3 = jnp.concatenate([u1, u1, u1], axis=0)
            term = lax.dot_general(ra3, u3, (((0,), (0,)), ((), ())), preferred_element_type=F32)
            acc[k, :, cols] = acc[k, :, cols] + crecv[k, :, cols].astype(F32) + term

    for k in range(2):
        for cs in range(2):
            remote(xsend.at[0], xrecv.at[k, cs], x_s.at[0], x_r.at[k, cs], partner).wait_recv()
            cols = pl.ds(cs * half, half)
            out[pl.ds(k * 128, 128), cols] = acc[k, :, cols] + xrecv[k, cs].astype(F32)

    all_sent(yrow.at[pl.ds(1, Y * XLO - 1)], y_s.at[0])
    all_sent(rs_send, z_s.at[0])
    all_sent(gbuf.at[0, pl.ds(1, Z - 1)], g_s.at[0])
    all_sent(gbuf.at[pl.ds(1, Y - 1)], f_s.at[0])
    all_sent(psend, p_s.at[0])
    all_sent(xsend, x_s.at[0])
    all_sent(csend, c_s.at[0])
    all_sent(rsend, ra_s.at[0])
    all_sent(usend, u_s.at[0])


def body(
    queries, fresh_keys, fresh_values, paged_keys, paged_values, request_page_table,
    live_token_count, request_adapter_slot, adapters_in_use, adapter_pool_row,
    adapter_down_factors, adapter_up_factors, output_weight, gating,
):
    rows, width = queries.shape
    n_out = output_weight.shape[1]
    half = n_out // 2
    hbm = pl.BlockSpec(memory_space=pltpu.HBM)
    smem = pl.BlockSpec(memory_space=pltpu.SMEM)
    V = pltpu.VMEM
    dma = pltpu.SemaphoreType.DMA
    one = dma((1,))
    def pinned(*xs):
        return [pltpu.with_memory_space_constraint(x, pltpu.HBM) for x in xs]

    total = pl.pallas_call(
        kernel,
        out_shape=jax.ShapeDtypeStruct((rows // 4, n_out), F32),
        in_specs=[hbm] * 8 + [smem] * 5,
        out_specs=pl.BlockSpec(memory_space=V),
        scratch_shapes=[
            V((rows, width), BF), V((rows, width), BF), V((rows, width), BF),
            V(paged_keys.shape, BF), V(paged_values.shape, BF), V((width, n_out), BF),
            V((2, 128, 1152), F32), V((2, 128, 1152), BF), V((8, 128, width), BF),
            V((4, 128, half), BF), V((4, 128, half), BF), V((4, 128, half), F32), V((4, 128, half), BF),
            V((2, 128, n_out), BF), V((2, 128, n_out), BF), V((2, 128, n_out), F32),
            V((2, 2, 128, half), BF),
            V((Y * XLO, 2 * RANK, width), BF), V((Z - 1, RANK, width), BF), V((Z, RANK, width), BF),
            V((Y, Z, RANK, width), BF),
            V((4, 2, RANK, 128), F32), V((4, 2, RANK, width), BF),
            V((3, 2, RANK, 128), F32), V((3, 2, RANK, width), BF),
            dma((15,)),
            one, dma((4, 2)), one, dma((2, 2)), one, one, one, one, one, one,
            one, dma((Z,)), one, one, one, one, one, one,
        ],
        compiler_params=pltpu.CompilerParams(
            collective_id=0, has_side_effects=True, vmem_limit_bytes=48 * 1024 * 1024
        ),
        name="attend_project",
    )(
        *pinned(
            queries, fresh_keys, fresh_values, paged_keys, paged_values,
            adapter_down_factors, adapter_up_factors, output_weight,
            request_page_table, live_token_count, request_adapter_slot, adapters_in_use, adapter_pool_row,
        )
    )
    gate = lax.dynamic_slice_in_dim(gating, lax.axis_index("tp") * 2, 2, 0)
    gated = gate[:, None, :] * total.reshape(2, -1, n_out)
    return gated.reshape(-1, n_out).astype(BF)


def solution(mesh):
    return jax.shard_map(
        body,
        mesh=mesh,
        in_specs=(
            P("req", "tp"), P("req", "tp"), P("req", "tp"),
            P("req", None, "tp"), P("req", None, "tp"),
            P("req", None), P("req"), P("req"), P(), P(),
            P("req", None, "tp"), P("req", None, None), P("tp", None), P("req", None),
        ),
        out_specs=P(("req", "tp"), None),
        check_vma=False,
    )
```
